32 devices in a mesh: groups: 2 (over y), tm: 4 (over z), fsdp: 4 (over x, core).
Axes of the slice: x: 2, y: 2, z: 4, core: 2. Of those that a mesh axis runs over, the one named last changes fastest.
Arguments:
- query_proj: bfloat16 [8192, 1024], P(('groups', 'tm'), 'fsdp'), parts along dimension 0, may hold values from -0.75 to 0.75
- key_proj: bfloat16 [8192, 1024], P(('groups', 'tm'), 'fsdp'), parts along dimension 0, may hold values from -0.75 to 0.75
- value_proj: bfloat16 [8192, 1024], P(('groups', 'tm'), 'fsdp'), parts along dimension 0, may hold values from -6 to 6
- log_decay: float32 [8192, 16], P(('groups', 'tm'), 'fsdp'), parts along dimension 0, may hold values from -0.5 to 0, as said below
- out_grad: bfloat16 [8192, 1024], P(('groups', 'tm'), 'fsdp'), parts along dimension 0, may hold values from -6 to 6
- out_weight: bfloat16 [1024, 1024], P('fsdp', 'tm'), may hold values from -0.1875 to 0.1875
Outputs:
- query_grad: bfloat16 [8192, 1024], P(('groups', 'tm'), 'fsdp'), parts along dimension 0
- key_grad: bfloat16 [8192, 1024], P(('groups', 'tm'), 'fsdp'), parts along dimension 0
- value_grad: bfloat16 [8192, 1024], P(('groups', 'tm'), 'fsdp'), parts along dimension 0
- decay_grad: float32 [8192, 16], P(('groups', 'tm'), 'fsdp'), parts along dimension 0
- weight_grad: float32 [2048, 1024], P(('groups', 'fsdp'), 'tm'), parts along dimension 0
The draws below stay inside these ranges and needn't reach their ends.
There are 2 independent parts, one for each index of `groups`. The reference program is written for one: setup_inputs(seed, part) draws one part's arguments, and reference() takes and returns one part's arrays. A program takes and returns all parts, laid end to end along the dimension named above; an argument that names none is the same for every part. Nothing has to cross between parts.
Inputs may be any that keep to these rules, and one draw needn't show every extreme that they name: `log_decay`: each entry is the logarithm of one head's decay at one token.
All inputs are finite; a program needn't handle non-finite values.
Results may differ from the reference program's by a relative error of at most 0.0029.
Values may be sent and summed in bfloat16 or wider, within the bound.
No kernel may reach another device: no remote copies, remote signals or barrier semaphores. Data moves between devices by JAX's collectives and lax.ppermute only.
A program may use at most 128 MiB of HBM per device.

```python
import jax
import jax.numpy as jnp
from jax import lax

HEADS = 16
HEAD_DIM = 64
BLOCK = 128
TOK_DEV = 1024
D = 1024
STREAM_TOKENS = 4096


def draw_log_decay(key, part):
    key_rapid_heads, key_gradual_heads, key_brisk_heads, key_token_rows, key_tile_block, key_spike = jax.random.split(key, 6)
    fast_share = 0.45
    fast_heads = jax.random.bernoulli(key_rapid_heads, fast_share, (HEADS,))
    slow_rate = jnp.exp(jax.random.uniform(key_gradual_heads, (HEADS,), jnp.float32, jnp.log(0.05), jnp.log(0.5))) / STREAM_TOKENS
    quick_rate = jnp.exp(jax.random.uniform(key_brisk_heads, (HEADS,), jnp.float32, jnp.log(1.0 / 50.0), jnp.log(1.0 / 30.0)))
    head_decay_speed = jnp.where(fast_heads, quick_rate, slow_rate)
    token_multiplier = jnp.exp(jax.random.uniform(key_token_rows, (STREAM_TOKENS, HEADS), jnp.float32, -0.69, 0.69))
    block_multiplier = jnp.exp(jax.random.uniform(key_tile_block, (STREAM_TOKENS // TOK_DEV, HEADS), jnp.float32, -0.69, 0.69))
    block_multiplier = jnp.repeat(block_multiplier, TOK_DEV, axis=0)
    spike_positions = jax.random.randint(key_spike, (3,), 0, STREAM_TOKENS)
    spike_rows = jnp.any(jnp.arange(STREAM_TOKENS)[:, None] == spike_positions[None, :], axis=1)
    return -(head_decay_speed[None, :] * token_multiplier * block_multiplier) - 0.35 * spike_rows[:, None].astype(jnp.float32)


def strengthened(drawn, rng, source, target, parts, factor):
    def block_of(axis_at):
        return (jnp.arange(drawn.shape[axis_at]) // (drawn.shape[axis_at] // parts)).reshape((-1,) + (1,) * (drawn.ndim - 1 - axis_at))

    near = jax.random.permutation(rng, parts)[block_of(target)]
    second = (block_of(target) + parts // 2) % parts
    return jnp.where((block_of(source) == near) | (block_of(source) == second), factor * drawn, drawn)


def block_levels(stream_key, shape, cuts, least, top_value):
    factor_of, own = 1.0, jax.random.fold_in(stream_key, 6)
    for dim, blocks in cuts:
        draws = jnp.exp(jax.random.uniform(jax.random.fold_in(own, dim), (blocks,), jnp.float32, least / len(cuts), top_value / len(cuts)))
        factor_of = factor_of * jnp.repeat(draws, shape[dim] // blocks).reshape([-1 if axis == dim else 1 for axis in range(len(shape))])
    return factor_of


def gaussian(own_key, shape, spread, most, cuts=(), held_as=jnp.bfloat16):
    result = jax.random.normal(own_key, shape, jnp.float32) * spread
    if len(cuts) > 0:
        result = block_levels(own_key, shape, cuts, -0.22, 0.18) * result
    return jnp.clip(result, min=-most, max=most).astype(held_as)


def bell_draw_with(rng, extent, scale, most, pieces, heavy, dtype=jnp.bfloat16):
    values = scale * jax.random.normal(rng, extent, jnp.float32)
    if pieces:
        values = values * block_levels(rng, extent, pieces, -0.22, 0.18)
    return jnp.clip(strengthened(values, jax.random.fold_in(rng, 3), *heavy), -most, most).astype(dtype)


def setup_inputs(seed: int = 0, part: int = 0) -> dict:
    key_of = jax.random.split(jax.random.key(seed), 7)
    part_splits = jax.random.split(jax.random.fold_in(key_of[6], part), 7)
    return {
        "query_proj": gaussian(part_splits[0], (STREAM_TOKENS, D), 0.125, 0.75, ((0, 4), (1, 4))),
        "key_proj": gaussian(part_splits[1], (STREAM_TOKENS, D), 0.125, 0.75, ((0, 4), (1, 4))),
        "value_proj": gaussian(part_splits[2], (STREAM_TOKENS, D), 1.0, 6.0, ((0, 4), (1, 4))),
        "log_decay": draw_log_decay(jax.random.fold_in(jax.random.fold_in(key_of[6], part), 71), part),
        "out_grad": bell_draw_with(part_splits[4], (STREAM_TOKENS, D), 1.0, 6.0, ((0, 4), (1, 4)), (0, 1, 4, 2.0)),
        "out_weight": gaussian(key_of[5], (D, D), D ** -0.5, 0.1875, ((0, 4), (1, 4))),
    }


def masked_exp(expo, keep):
    return jnp.where(keep, jnp.exp(jnp.where(keep, expo, 0.0)), 0.0)


def block_scores(query_blk, key_blk, value_blk, grad_blk, cum_blk):
    high = lax.Precision.HIGHEST
    lower_mask = jnp.tril(jnp.ones((BLOCK, BLOCK), bool))
    pair_weights = masked_exp(cum_blk[:, :, None] - cum_blk[:, None, :], lower_mask)
    scores = jnp.einsum("hie,hje->hij", query_blk, key_blk, precision=high) * pair_weights
    grad_scores = jnp.einsum("hie,hje->hij", grad_blk, value_blk, precision=high) * pair_weights
    return scores, grad_scores


def reference(query_proj, key_proj, value_proj, log_decay, out_grad, out_weight):
    high = lax.Precision.HIGHEST
    inner_grad = jnp.dot(out_grad, out_weight.T, preferred_element_type=jnp.float32)
    block_total = STREAM_TOKENS // BLOCK

    def split_heads(matrix):
        return matrix.astype(jnp.float32).reshape(block_total, BLOCK, HEADS, HEAD_DIM).transpose(0, 2, 1, 3)

    def join_heads(blocks):
        return blocks.transpose(0, 2, 1, 3).reshape(STREAM_TOKENS, D)

    queries = split_heads(query_proj)
    keys_all = split_heads(key_proj)
    values = split_heads(value_proj)
    grads = split_heads(inner_grad)
    decay = log_decay.reshape(block_total, BLOCK, HEADS).transpose(0, 2, 1)
    zero_state = jnp.zeros((HEADS, HEAD_DIM, HEAD_DIM), jnp.float32)

    def forward_step(state, inputs):
        query_blk, key_blk, value_blk, grad_blk, decay_blk = inputs
        cum_blk = jnp.cumsum(decay_blk, axis=1)
        total_blk = cum_blk[:, -1]
        scores, grad_scores = block_scores(query_blk, key_blk, value_blk, grad_blk, cum_blk)
        grow = jnp.exp(cum_blk)[:, :, None]
        shrink = jnp.exp(total_blk[:, None] - cum_blk)[:, :, None]
        out_blk = jnp.einsum("hij,hje->hie", scores, value_blk, precision=high) + grow * jnp.einsum("hbi,hij->hbj", query_blk, state, precision=high)
        qgrad_blk = jnp.einsum("hij,hje->hie", grad_scores, key_blk, precision=high) + grow * jnp.einsum("hbj,hij->hbi", grad_blk, state, precision=high)
        new_state = jnp.exp(total_blk)[:, None, None] * state + jnp.einsum("hbi,hbj->hij", key_blk * shrink, value_blk, precision=high)
        return new_state, (out_blk, qgrad_blk)

    def backward_step(back, inputs):
        query_blk, key_blk, value_blk, grad_blk, decay_blk = inputs
        cum_blk = jnp.cumsum(decay_blk, axis=1)
        total_blk = cum_blk[:, -1]
        scores, grad_scores = block_scores(query_blk, key_blk, value_blk, grad_blk, cum_blk)
        grow = jnp.exp(cum_blk)[:, :, None]
        shrink = jnp.exp(total_blk[:, None] - cum_blk)[:, :, None]
        kgrad_blk = jnp.einsum("hij,hie->hje", grad_scores, query_blk, precision=high) + shrink * jnp.einsum("hbj,hij->hbi", value_blk, back, precision=high)
        vgrad_blk = jnp.einsum("hij,hie->hje", scores, grad_blk, precision=high) + shrink * jnp.einsum("hbi,hij->hbj", key_blk, back, precision=high)
        new_back = jnp.exp(total_blk)[:, None, None] * back + jnp.einsum("hbi,hbj->hij", query_blk * grow, grad_blk, precision=high)
        return new_back, (kgrad_blk, vgrad_blk)

    inputs = (queries, keys_all, values, grads, decay)
    final_state, (outputs, query_full) = lax.scan(forward_step, zero_state, inputs)
    final_back, (key_full, value_full) = lax.scan(backward_step, zero_state, inputs, reverse=True)
    outputs_low = join_heads(outputs).astype(jnp.bfloat16)
    weight_grad = jnp.dot(outputs_low.T, out_grad, preferred_element_type=jnp.float32)
    decay_terms = jnp.sum(queries * query_full - keys_all * key_full, axis=3)
    decay_terms = decay_terms.transpose(0, 2, 1).reshape(STREAM_TOKENS, HEADS)
    decay_grad = jnp.flip(jnp.cumsum(jnp.flip(decay_terms, 0), axis=0), 0)
    return (join_heads(query_full).astype(jnp.bfloat16), join_heads(key_full).astype(jnp.bfloat16), join_heads(value_full).astype(jnp.bfloat16), decay_grad, weight_grad)
```

```python
import functools

import jax
import jax.numpy as jnp
from jax import lax
from jax.experimental import pallas as pl
from jax.experimental.pallas import tpu as pltpu
from jax.sharding import PartitionSpec as P

HEAD_DIM = 64
BLOCK = 128
PAD = 8

F32 = jnp.float32
BF16 = jnp.bfloat16
NN = (((1,), (0,)), ((), ()))
NT = (((1,), (1,)), ((), ()))


def mm(a, b, dims=NN):
    return lax.dot_general(a, b, dims, preferred_element_type=F32)


def split2(x):
    high = x.astype(BF16)
    return high, (x - high.astype(F32)).astype(BF16)


def split3(x):
    high = x.astype(BF16)
    rest = x - high.astype(F32)
    mid = rest.astype(BF16)
    return high, mid, (rest - mid.astype(F32)).astype(BF16)


def iota(shape, axis):
    return lax.broadcasted_iota(jnp.int32, shape, axis)


def ones_where(keep):
    return jnp.where(keep, 1.0, 0.0).astype(BF16)


def spread(heads, width):
    lanes = heads * width
    return ones_where(iota((heads, lanes), 1) // width == iota((heads, lanes), 0))


def compact(full, heads):
    lanes = full.shape[1]
    head_of = iota((HEAD_DIM, lanes), 1) // HEAD_DIM
    out = jnp.zeros((HEAD_DIM, lanes), F32)
    for h in range(heads):
        out = jnp.where(head_of == h, full[h * HEAD_DIM : (h + 1) * HEAD_DIM, :], out)
    return out


def expand(state, heads):
    lanes = state.shape[1]
    full = jnp.concatenate([state] * heads, axis=0)
    keep = iota((lanes, lanes), 0) // HEAD_DIM == iota((lanes, lanes), 1) // HEAD_DIM
    return jnp.where(keep, full, 0.0)


def stacked(block, heads):
    head_of = iota(block.shape, 1) // HEAD_DIM
    zero = jnp.zeros_like(block)
    return jnp.concatenate([jnp.where(head_of == h, block, zero) for h in range(heads)], axis=0)


def rows_of(b):
    return pl.ds(pl.multiple_of(b * BLOCK, BLOCK), BLOCK)


def summary_kernel(heads, blocks, decay, key, value, ccol, crow, cexp, state_blocks, message):
    lanes = heads * HEAD_DIM
    lower = ones_where(iota((BLOCK, BLOCK), 0) >= iota((BLOCK, BLOCK), 1))
    to_lanes = spread(heads, HEAD_DIM)
    pick = ones_where(iota((PAD, heads), 0) == iota((PAD, heads), 1))

    def step(b, carry):
        state, total = carry
        rows = rows_of(b)
        cum = sum(mm(lower, part) for part in split3(decay[rows, :]))
        parts = split3(cum)
        wide = sum(mm(part, to_lanes) for part in parts)
        ccol[rows, :] = cum
        crow[b] = sum(mm(pick, part, NT) for part in parts)
        cexp[rows, :] = wide
        block_total = wide[BLOCK - 1 :, :]
        shrunk = value[rows, :].astype(F32) * jnp.exp(block_total - wide)
        key_t = key[rows, :].T
        block_state = compact(sum(mm(key_t, part) for part in split2(shrunk)), heads)
        state_blocks[b] = block_state
        return jnp.exp(block_total) * state + block_state, total + block_total

    state, total = lax.fori_loop(
        0, blocks, step, (jnp.zeros((HEAD_DIM, lanes), F32), jnp.zeros((1, lanes), F32))
    )
    message[:HEAD_DIM, :] = state
    message[HEAD_DIM:, :] = jnp.broadcast_to(total, (PAD, lanes))


def pair_weights(ccol_block, crow_block, heads, flipped):
    across = spread(heads, BLOCK)
    wide = sum(mm(part, across) for part in split3(ccol_block))
    row, col = iota((BLOCK, BLOCK), 0), iota((BLOCK, BLOCK), 1)
    keep = (row <= col) if flipped else (row >= col)
    out = []
    for h in range(heads):
        mine = wide[:, h * BLOCK : (h + 1) * BLOCK]
        other = crow_block[h : h + 1, :]
        expo = (other - mine) if flipped else (mine - other)
        out.append(jnp.where(keep, jnp.exp(expo), 0.0))
    return jnp.concatenate(out, axis=1)


def inside_kernel(heads, blocks, query, key, value, ccol, crow, out):
    def step(b, carry):
        rows = rows_of(b)
        weights = pair_weights(ccol[rows, :], crow[b], heads, False)
        scores = mm(query[rows, :], stacked(key[rows, :], heads), NT) * weights
        values = stacked(value[rows, :], heads)
        out[rows, :] = sum(mm(part, values) for part in split2(scores))
        return carry

    lax.fori_loop(0, blocks, step, 0)


def output_kernel(heads, blocks, query, cexp, inside, state_in, state_blocks, out_t, states):
    def step(b, state):
        rows = rows_of(b)
        states[b] = state
        wide = cexp[rows, :]
        carried = sum(mm(query[rows, :], part) for part in split2(expand(state, heads)))
        block_out = (inside[rows, :] + jnp.exp(wide) * carried).astype(BF16)
        out_t[:, rows] = block_out.T
        return jnp.exp(wide[BLOCK - 1 :, :]) * state + state_blocks[b]

    states[blocks] = lax.fori_loop(0, blocks, step, state_in[...])


def inner_kernel(heads, blocks, count, refs):
    swap = refs[0]
    weights = refs[1 : 1 + count]
    columns = refs[1 + count : 1 + 2 * count]
    query, cexp, grad_high, grad_low, back_blocks, message, held, total = refs[1 + 2 * count :]
    lanes = heads * HEAD_DIM
    for k in range(count):
        held[k] = weights[k][...]
    for j in range(count):
        part = mm(columns[j][...], held[swap[0] ^ j], NT)
        total[...] = part if j == 0 else total[...] + part

    def step(i, carry):
        back, decayed = carry
        b = blocks - 1 - i
        rows = rows_of(b)
        wide = cexp[rows, :]
        grad = total[rows, :]
        high, low = split2(grad)
        grad_high[rows, :] = high
        grad_low[rows, :] = low
        query_t = query[rows, :].T
        grown = split2(grad * jnp.exp(wide))
        block_back = compact(sum(mm(query_t, part) for part in grown), heads)
        back_blocks[b] = block_back
        block_total = wide[BLOCK - 1 :, :]
        return jnp.exp(block_total) * back + block_back, decayed + block_total

    back, decayed = lax.fori_loop(
        0, blocks, step, (jnp.zeros((HEAD_DIM, lanes), F32), jnp.zeros((1, lanes), F32))
    )
    message[:HEAD_DIM, :] = back
    message[HEAD_DIM:, :] = jnp.broadcast_to(decayed, (PAD, lanes))


def weight_kernel(count, refs):
    swap, out_t = refs[:2]
    columns = refs[2 : 2 + count]
    outs = refs[2 + count : 2 + 2 * count]
    held = refs[2 + 2 * count]
    for j in range(count):
        held[j] = mm(out_t[...], columns[j][...])
    for k in range(count):
        outs[k][...] = held[swap[0] ^ k].astype(outs[k].dtype)


def head_sums(terms, heads):
    lanes = terms.shape[1]
    gather = ones_where(
        iota((lanes, heads), 0) // HEAD_DIM == iota((lanes, heads), 1)
    )
    return sum(mm(part, gather) for part in split3(terms))


def grads_kernel(
    heads, blocks, query, key, value, grad_high, grad_low, ccol, crow, cexp, states,
    query_grad, query_terms, key_inside, value_inside,
):
    def step(b, carry):
        rows = rows_of(b)
        q, k, v = query[rows, :], key[rows, :], value[rows, :]
        gh, gl = grad_high[rows, :], grad_low[rows, :]
        ccol_block, crow_block = ccol[rows, :], crow[b]
        q_stack, k_stack, v_stack = stacked(q, heads), stacked(k, heads), stacked(v, heads)
        gh_stack, gl_stack = stacked(gh, heads), stacked(gl, heads)
        weights = pair_weights(ccol_block, crow_block, heads, False)
        grad_scores = (mm(gh, v_stack, NT) + mm(gl, v_stack, NT)) * weights
        state_high, state_low = split2(expand(states[b], heads))
        carried = mm(gh, state_high, NT) + mm(gh, state_low, NT) + mm(gl, state_high, NT)
        full = jnp.exp(cexp[rows, :]) * carried
        full = full + sum(mm(part, k_stack) for part in split2(grad_scores))
        query_grad[rows, :] = full.astype(BF16)
        query_terms[rows, :] = head_sums(q.astype(F32) * full, heads)
        flipped = pair_weights(ccol_block, crow_block, heads, True)
        scores_t = mm(k, q_stack, NT) * flipped
        high, low = split2(scores_t)
        value_inside[rows, :] = mm(high, gh_stack) + mm(high, gl_stack) + mm(low, gh_stack)
        grad_t = (mm(v, gh_stack, NT) + mm(v, gl_stack, NT)) * flipped
        key_inside[rows, :] = sum(mm(part, q_stack) for part in split2(grad_t))
        return carry

    lax.fori_loop(0, blocks, step, 0)


def final_kernel(
    heads, blocks, key, value, cexp, states, back_in, back_blocks, query_terms, key_inside,
    value_inside, key_grad, value_grad, decay_grad,
):
    upper = ones_where(iota((BLOCK, BLOCK), 0) <= iota((BLOCK, BLOCK), 1))

    def step(i, back):
        b = blocks - 1 - i
        rows = rows_of(b)
        k, v = key[rows, :], value[rows, :]
        wide = cexp[rows, :]
        block_total = wide[BLOCK - 1 :, :]
        shrink = jnp.exp(block_total - wide)
        back_high, back_low = split2(expand(back, heads))
        key_full = key_inside[rows, :] + shrink * (mm(v, back_high, NT) + mm(v, back_low, NT))
        value_full = value_inside[rows, :] + shrink * (mm(k, back_high) + mm(k, back_low))
        key_grad[rows, :] = key_full.astype(BF16)
        value_grad[rows, :] = value_full.astype(BF16)
        terms = query_terms[rows, :] - head_sums(k.astype(F32) * key_full, heads)
        tail = jnp.sum(states[b + 1] * back, axis=0, keepdims=True)
        tail = head_sums(jnp.broadcast_to(tail, (PAD, tail.shape[1])), heads)
        decay_grad[rows, :] = sum(mm(upper, part) for part in split3(terms)) + tail[:1, :]
        return jnp.exp(block_total) * back + back_blocks[b]

    lax.fori_loop(0, blocks, step, back_in[...])


def shape(dims, dtype=F32):
    return jax.ShapeDtypeStruct(dims, dtype)


def call(kernel, outs, scalars=0, scratch=(), name=None):
    def run(*args):
        smem = pl.BlockSpec(memory_space=pltpu.SMEM)
        vmem = pl.BlockSpec(memory_space=pltpu.VMEM)
        return pl.pallas_call(
            kernel,
            out_shape=outs,
            in_specs=[smem] * scalars + [vmem] * (len(args) - scalars),
            out_specs=jax.tree.map(lambda _: vmem, outs),
            scratch_shapes=list(scratch),
            name=name,
        )(*args)

    return run


def swap_with(value, axis, size, mask):
    return lax.ppermute(value, axis, [(i, i ^ mask) for i in range(size)])


def prefix_states(message, axis, size, index, ahead):
    group, total = message[:HEAD_DIM], message[HEAD_DIM : HEAD_DIM + 1]
    inside, inside_total = jnp.zeros_like(group), jnp.zeros_like(total)
    mask = 1
    while mask < size:
        other = swap_with(message, axis, size, mask)
        other_group, other_total = other[:HEAD_DIM], other[HEAD_DIM : HEAD_DIM + 1]
        mine_later = (index & mask) != 0
        takes = mine_later if ahead else jnp.logical_not(mine_later)
        inside = jnp.where(takes, inside + jnp.exp(inside_total) * other_group, inside)
        inside_total = jnp.where(takes, inside_total + other_total, inside_total)
        mask *= 2
        if mask < size:
            group = jnp.where(
                takes,
                jnp.exp(total) * other_group + group,
                jnp.exp(other_total) * group + other_group,
            )
            total = total + other_total
            message = jnp.concatenate([group, jnp.broadcast_to(total, (PAD, total.shape[1]))], 0)
    return inside


def local(sizes, query, key, value, decay, out_grad, out_weight):
    tm, fsdp = sizes
    rows, lanes = query.shape
    heads = lanes // HEAD_DIM
    blocks = rows // BLOCK
    mine, column = lax.axis_index("tm"), lax.axis_index("fsdp")
    direct = tm == fsdp and tm & (tm - 1) == 0

    columns = [out_grad]
    mask = fsdp // 2
    steps = []
    while mask:
        steps.append(mask)
        mask //= 2
    order = {0: out_grad}
    for mask in steps:
        for held in list(order):
            order[held | mask] = swap_with(order[held], "fsdp", fsdp, mask)
    columns = [order[j] for j in range(fsdp)]

    if direct:
        weights = [out_weight] + [swap_with(out_weight, "tm", tm, k) for k in range(1, tm)]
        swap = mine ^ column
    else:
        whole = lax.all_gather(out_weight, "tm", axis=1, tiled=True)
        weights = jnp.split(whole, fsdp, axis=1)
        swap = column
    swap = jnp.reshape(swap, (1,)).astype(jnp.int32)

    ccol, crow, cexp, state_blocks, message = call(
        functools.partial(summary_kernel, heads, blocks),
        (
            shape((rows, heads)),
            shape((blocks, PAD, BLOCK)),
            shape((rows, lanes)),
            shape((blocks, HEAD_DIM, lanes)),
            shape((HEAD_DIM + PAD, lanes)),
        ),
        name="summary",
    )(decay, key, value)
    state_in = prefix_states(message, "tm", tm, mine, True)
    inside = call(
        functools.partial(inside_kernel, heads, blocks), shape((rows, lanes)), name="inside"
    )(query, key, value, ccol, crow)
    out_t, states = call(
        functools.partial(output_kernel, heads, blocks),
        (shape((lanes, rows), BF16), shape((blocks + 1, HEAD_DIM, lanes))),
        name="outputs",
    )(query, cexp, inside, state_in, state_blocks)

    width = out_grad.shape[1]
    sent = BF16 if direct else F32
    partials = call(
        lambda *refs: weight_kernel(fsdp, refs),
        tuple(shape((lanes, width), F32 if k == 0 else sent) for k in range(fsdp)),
        scalars=1,
        scratch=[pltpu.VMEM((fsdp, lanes, width), F32)],
        name="weight",
    )(swap, out_t, *columns)
    if direct:
        weight_grad = partials[0]
        for k in range(1, tm):
            weight_grad = weight_grad + swap_with(partials[k], "tm", tm, k).astype(F32)
    else:
        weight_grad = lax.psum_scatter(
            jnp.concatenate(partials, axis=1), "tm", scatter_dimension=1, tiled=True
        )

    grad_high, grad_low, back_blocks, message = call(
        lambda *refs: inner_kernel(heads, blocks, fsdp, refs),
        (
            shape((rows, lanes), BF16),
            shape((rows, lanes), BF16),
            shape((blocks, HEAD_DIM, lanes)),
            shape((HEAD_DIM + PAD, lanes)),
        ),
        scalars=1,
        scratch=[pltpu.VMEM((fsdp, lanes, width), BF16), pltpu.VMEM((rows, lanes), F32)],
        name="inner",
    )(swap, *weights, *columns, query, cexp)
    back_in = prefix_states(message, "tm", tm, mine, False)

    query_grad, query_terms, key_inside, value_inside = call(
        functools.partial(grads_kernel, heads, blocks),
        (
            shape((rows, lanes), BF16),
            shape((rows, heads)),
            shape((rows, lanes)),
            shape((rows, lanes)),
        ),
        name="grads",
    )(query, key, value, grad_high, grad_low, ccol, crow, cexp, states)
    key_grad, value_grad, decay_grad = call(
        functools.partial(final_kernel, heads, blocks),
        (shape((rows, lanes), BF16), shape((rows, lanes), BF16), shape((rows, heads))),
        name="final",
    )(
        key, value, cexp, states, back_in, back_blocks, query_terms, key_inside, value_inside,
    )
    return query_grad, key_grad, value_grad, decay_grad, weight_grad


def solution(mesh):
    wide = P(("groups", "tm"), "fsdp")
    sizes = (mesh.shape["tm"], mesh.shape["fsdp"])
    return jax.shard_map(
        functools.partial(local, sizes),
        mesh=mesh,
        in_specs=(wide, wide, wide, wide, wide, P("fsdp", "tm")),
        out_specs=(wide, wide, wide, wide, P(("groups", "fsdp"), "tm")),
        check_vma=False,
    )
```

```python
import functools

import jax
import jax.numpy as jnp
from jax import lax
from jax.experimental import pallas as pl
from jax.experimental.pallas import tpu as pltpu
from jax.sharding import PartitionSpec as P

HEAD_DIM = 64
BLOCK = 128
PAD = 8
PAIR = 2 * HEAD_DIM
LOG2_E = 1.4426950408889634

F32 = jnp.float32
BF16 = jnp.bfloat16
NN = (((1,), (0,)), ((), ()))
NT = (((1,), (1,)), ((), ()))

GRANT = 24 << 20
COST = {
    "summary": 3, "inside": 4, "outputs": 4, "weight": 2, "inner": 4, "grads": 10, "final": 4,
}


def mm(a, b, dims=NN):
    return lax.dot_general(a, b, dims, preferred_element_type=F32)


def split2(x):
    high = x.astype(BF16)
    return high, (x - high.astype(F32)).astype(BF16)


def split3(x):
    high = x.astype(BF16)
    rest = x - high.astype(F32)
    mid = rest.astype(BF16)
    return high, mid, (rest - mid.astype(F32)).astype(BF16)


def iota(shape, axis):
    return lax.broadcasted_iota(jnp.int32, shape, axis)


def ones_where(keep):
    return jnp.where(keep, 1.0, 0.0).astype(BF16)


def cat(parts, axis):
    return jnp.concatenate(parts, axis=axis)


def rows_of(b):
    return pl.ds(b * BLOCK, BLOCK)


def loop(blocks, step, carry):
    for b in range(blocks):
        carry = step(b, carry)
    return carry


def lanes_of(p):
    return slice(p * PAIR, (p + 1) * PAIR)


def first_head(like):
    return iota(like.shape, 1) < HEAD_DIM


def stacked(pair):
    keep, zero = first_head(pair), jnp.zeros_like(pair)
    return cat([jnp.where(keep, pair, zero), jnp.where(keep, zero, pair)], 0)


def spread_heads(both):
    count = both.shape[1] // PAIR
    zero = jnp.zeros((2 * both.shape[0], PAIR), both.dtype)
    out = []
    for p in range(count):
        row = [zero] * count
        row[p] = stacked(both[:, lanes_of(p)])
        out.append(cat(row, 1))
    return cat(out, 0)


def compact(full):
    out = []
    for p in range(full.shape[1] // PAIR):
        mine = full[lanes_of(p), lanes_of(p)]
        top = mine[:HEAD_DIM, :]
        out.append(jnp.where(first_head(top), top, mine[HEAD_DIM:, :]))
    return cat(out, 1)


def columns_of(by_token, b):
    return by_token[:, b * PAD : (b + 1) * PAD]


def wide_all(columns, heads):
    return cat([wide_of(columns, p) for p in range(heads // 2)], 1)


def wide_of(columns, p):
    one, two = columns[:, 2 * p : 2 * p + 1], columns[:, 2 * p + 1 : 2 * p + 2]
    keep = iota((BLOCK, PAIR), 1) < HEAD_DIM
    return jnp.where(
        keep, jnp.broadcast_to(one, (BLOCK, PAIR)), jnp.broadcast_to(two, (BLOCK, PAIR))
    )


def exponents(columns, crow_block, p):
    return [
        jnp.broadcast_to(columns[:, h : h + 1], (BLOCK, BLOCK)) - crow_block[h : h + 1, :]
        for h in (2 * p, 2 * p + 1)
    ]


def pair_weights(expos, flipped):
    row, col = iota((BLOCK, BLOCK), 0), iota((BLOCK, BLOCK), 1)
    keep = (row <= col) if flipped else (row >= col)
    return cat([jnp.where(keep, jnp.exp2(-e if flipped else e), 0.0) for e in expos], 1)


def fold(both):
    half = both.shape[0] // 2
    return both[:half, :] + both[half:, :]


def wide_state(state):
    high, low = split2(state)
    return spread_heads(high), spread_heads(low)


def takes_from(mask, ahead):
    later = (lax.axis_index("tm") & mask) != 0
    return later if ahead else jnp.logical_not(later)


def entering(takes, inside, other):
    state, total = inside[:HEAD_DIM, :], inside[HEAD_DIM : HEAD_DIM + 1, :]
    return jnp.where(takes, state + jnp.exp2(total) * other[:HEAD_DIM, :], state)


def summary_kernel(heads, blocks, decay, key, value, crow, ccol, state_blocks, message):
    lanes = heads * HEAD_DIM
    upper = ones_where(iota((BLOCK, BLOCK), 0) <= iota((BLOCK, BLOCK), 1))
    filler = [jnp.zeros((PAD - heads, BLOCK), F32)] if heads < PAD else []
    rates = cat([cat([decay[:, rows_of(b)]] + filler, 0) for b in range(blocks)], 0) * LOG2_E
    sums = mm(cat(split3(rates), 0), upper)
    size = blocks * PAD
    cum = sums[:size, :] + sums[size : 2 * size, :] + sums[2 * size :, :]
    by_token = cum.T
    ccol[...] = by_token
    state, total = jnp.zeros((HEAD_DIM, lanes), F32), jnp.zeros((1, lanes), F32)
    for b in range(blocks):
        rows = rows_of(b)
        crow[b] = cum[b * PAD : (b + 1) * PAD, :]
        columns = columns_of(by_token, b)
        wide = wide_all(columns, heads)
        block_total = wide[BLOCK - 1 :, :]
        shrunk = value[rows, :].astype(F32) * jnp.exp2(block_total - wide)
        key_t = key[rows, :].T
        block_state = compact(mm(cat([key_t, key_t], 1), cat(split2(shrunk), 0)))
        state_blocks[b] = block_state
        state = jnp.exp2(block_total) * state + block_state
        total = total + block_total
    message[:HEAD_DIM, :] = state
    message[HEAD_DIM:, :] = jnp.broadcast_to(total, (PAD, lanes))


def inside_kernel(heads, blocks, query, key, value, crow, ccol, out):
    def step(b, carry):
        rows = rows_of(b)
        crow_block = crow[b]
        columns = columns_of(ccol, b)
        scores = []
        for p in range(heads // 2):
            side = lanes_of(p)
            weights = pair_weights(exponents(columns, crow_block, p), False)
            scores.append(mm(query[rows, side], stacked(key[rows, side]), NT) * weights)
        out[rows, :] = fold(mm(cat(split2(cat(scores, 1)), 0), spread_heads(value[rows, :])))
        return carry

    loop(blocks, step, 0)


def output_kernel(
    heads, blocks, mask, query, ccol, inside, before, other, state_blocks, out_t, states
):
    def step(b, state):
        rows = rows_of(b)
        states[b] = state
        columns = columns_of(ccol, b)
        wide = wide_all(columns, heads)
        q = query[rows, :]
        carried = mm(cat([q, q], 1), cat(wide_state(state), 0))
        block_out = (inside[rows, :] + jnp.exp2(wide) * carried).astype(BF16)
        out_t[:, rows] = block_out.T
        return jnp.exp2(wide[BLOCK - 1 :, :]) * state + state_blocks[b]

    first = entering(takes_from(mask, True), before, other)
    states[blocks] = loop(blocks, step, first)


def swap_of(direct):
    column = lax.axis_index("fsdp")
    return lax.axis_index("tm") ^ column if direct else column


def inner_kernel(heads, blocks, count, direct, refs):
    swap = swap_of(direct)
    weights = refs[:count]
    columns_in = refs[count : 2 * count]
    query, ccol, grad_high, grad_low, back_blocks, message, held, total = refs[2 * count :]
    lanes = heads * HEAD_DIM
    for k in range(count):
        held[k] = weights[k][...]
    for j in range(count):
        part = mm(columns_in[j][...], held[swap ^ j], NT)
        total[...] = part if j == 0 else total[...] + part

    def step(i, carry):
        back, decayed = carry
        b = blocks - 1 - i
        rows = rows_of(b)
        columns = columns_of(ccol, b)
        wide = wide_all(columns, heads)
        block_total = wide[BLOCK - 1 :, :]
        grad = total[rows, :]
        high, low = split2(grad)
        grad_high[rows, :] = high
        grad_low[rows, :] = low
        query_t = query[rows, :].T
        grown = split2(grad * jnp.exp2(wide))
        block_back = compact(mm(cat([query_t, query_t], 1), cat(grown, 0)))
        back_blocks[b] = block_back
        return jnp.exp2(block_total) * back + block_back, decayed + block_total

    carry = (jnp.zeros((HEAD_DIM, lanes), F32), jnp.zeros((1, lanes), F32))
    back, decayed = loop(blocks, step, carry)
    message[:HEAD_DIM, :] = back
    message[HEAD_DIM:, :] = jnp.broadcast_to(decayed, (PAD, lanes))


def weight_kernel(count, direct, refs):
    swap = swap_of(direct)
    out_t = refs[0]
    columns = refs[1 : 1 + count]
    outs = refs[1 + count : 1 + 2 * count]
    held = refs[1 + 2 * count]
    for j in range(count):
        held[j] = mm(out_t[...], columns[j][...])
    for k in range(count):
        outs[k][...] = held[swap ^ k].astype(outs[k].dtype)


def head_rows(terms):
    lanes = terms.shape[1]
    pick = ones_where(iota((PAD, lanes), 1) // HEAD_DIM == iota((PAD, lanes), 0))
    return mm(cat([pick, pick], 1), cat(split2(terms), 1), NT)


def grads_kernel(
    heads, blocks, query, key, value, grad_high, grad_low, crow, ccol, states,
    query_grad, query_terms, key_inside, value_inside,
):
    def step(b, carry):
        rows = rows_of(b)
        crow_block = crow[b]
        columns = columns_of(ccol, b)
        q, k, v = query[rows, :], key[rows, :], value[rows, :]
        gh, gl = grad_high[rows, :], grad_low[rows, :]
        grad_scores, scores_t, grad_t = [], [], []
        for p in range(heads // 2):
            side = lanes_of(p)
            gh_pair, gl_pair, v_pair = gh[:, side], gl[:, side], v[:, side]
            gh_stack, gl_stack, v_stack = stacked(gh_pair), stacked(gl_pair), stacked(v_pair)
            expos = exponents(columns, crow_block, p)
            weights = pair_weights(expos, False)
            flipped = pair_weights(expos, True)
            both = cat([gh_pair, gl_pair], 1)
            grad_scores.append(mm(both, cat([v_stack, v_stack], 1), NT) * weights)
            scores_t.append(mm(k[:, side], stacked(q[:, side]), NT) * flipped)
            both = cat([gh_stack, gl_stack], 1)
            grad_t.append(mm(cat([v_pair, v_pair], 1), both, NT) * flipped)
        state_high, state_low = wide_state(states[b])
        carried = mm(cat([gh, gl, gh], 1), cat([state_high, state_high, state_low], 1), NT)
        full = jnp.exp2(wide_all(columns, heads)) * carried
        full = full + fold(mm(cat(split2(cat(grad_scores, 1)), 0), spread_heads(k)))
        query_grad[rows, :] = full.astype(BF16)
        query_terms[b] = head_rows(q.astype(F32) * full)
        high, low = split2(cat(scores_t, 1))
        value_inside[rows, :] = fold(mm(cat([high, low], 0), spread_heads(gh))) + mm(
            high, spread_heads(gl)
        )
        key_inside[rows, :] = fold(mm(cat(split2(cat(grad_t, 1)), 0), spread_heads(q)))
        return carry

    loop(blocks, step, 0)


def final_kernel(
    heads, blocks, mask, key, value, ccol, states, before, other, back_blocks, query_terms,
    key_inside, value_inside, key_grad, value_grad, decay_grad, term_rows, tail_rows,
):
    lanes = heads * HEAD_DIM

    def step(i, back):
        b = blocks - 1 - i
        rows = rows_of(b)
        columns = columns_of(ccol, b)
        k, v = key[rows, :], value[rows, :]
        wide = wide_all(columns, heads)
        block_total = wide[BLOCK - 1 :, :]
        shrink = jnp.exp2(block_total - wide)
        back_high, back_low = wide_state(back)
        carried = mm(cat([v, v], 1), cat([back_high, back_low], 1), NT)
        key_full = key_inside[rows, :] + shrink * carried
        carried = mm(cat([k, k], 1), cat([back_high, back_low], 0))
        value_full = value_inside[rows, :] + shrink * carried
        key_grad[rows, :] = key_full.astype(BF16)
        value_grad[rows, :] = value_full.astype(BF16)
        terms = query_terms[b] - head_rows(k.astype(F32) * key_full)
        term_rows[b] = terms
        tail_rows[b] = jnp.broadcast_to(
            jnp.sum(states[b + 1] * back, axis=0, keepdims=True), (PAD, lanes)
        )
        return jnp.exp2(block_total) * back + back_blocks[b]

    loop(blocks, step, entering(takes_from(mask, False), before, other))
    lower = ones_where(iota((BLOCK, BLOCK), 0) >= iota((BLOCK, BLOCK), 1))
    terms = cat([term_rows[b] for b in range(blocks)], 0)
    sums = mm(cat(split3(terms), 0), lower)
    size = blocks * PAD
    sums = sums[:size, :] + sums[size : 2 * size, :] + sums[2 * size :, :]
    tails = cat([tail_rows[b] for b in range(blocks)], 0)
    pick = ones_where(iota((PAD, lanes), 1) // HEAD_DIM == iota((PAD, lanes), 0))
    ends = sum(mm(pick, part, NT) for part in split3(tails))
    for b in range(blocks):
        end = jnp.broadcast_to(ends[:, b * PAD : b * PAD + 1], (PAD, BLOCK))
        both = sums[b * PAD : (b + 1) * PAD, :] + end
        decay_grad[:, rows_of(b)] = both[:heads, :]


def combine_kernel(first, mask, ahead, mine, other, *refs):
    inside = None if first else refs[0]
    sent, kept = refs[-2:]
    takes = takes_from(mask, ahead)
    group, total = mine[:HEAD_DIM, :], mine[HEAD_DIM:, :]
    other_group, other_total = other[:HEAD_DIM, :], other[HEAD_DIM:, :]
    if first:
        state, decayed = jnp.zeros_like(group), jnp.zeros_like(total)
    else:
        state, decayed = inside[:HEAD_DIM, :], inside[HEAD_DIM:, :]
    kept[:HEAD_DIM, :] = jnp.where(takes, state + jnp.exp2(decayed[:1, :]) * other_group, state)
    kept[HEAD_DIM:, :] = jnp.where(takes, decayed + other_total, decayed)
    sent[:HEAD_DIM, :] = jnp.where(
        takes,
        jnp.exp2(total[:1, :]) * other_group + group,
        jnp.exp2(other_total[:1, :]) * group + other_group,
    )
    sent[HEAD_DIM:, :] = total + other_total


def shape(dims, dtype=F32):
    return jax.ShapeDtypeStruct(dims, dtype)


def call(kernel, outs, scratch=(), name=None):
    def run(*args):
        vmem = pl.BlockSpec(memory_space=pltpu.VMEM)
        return pl.pallas_call(
            kernel,
            out_shape=outs,
            in_specs=[vmem] * len(args),
            out_specs=jax.tree.map(lambda _: vmem, outs),
            scratch_shapes=list(scratch),
            compiler_params=pltpu.CompilerParams(vmem_limit_bytes=GRANT),
            cost_estimate=pl.CostEstimate(
                flops=COST.get(name, 1) * 1_000_000_000, bytes_accessed=0, transcendentals=0
            ),
            name=name,
        )(*args)

    return run


def swap_with(value, axis, size, mask):
    return lax.ppermute(value, axis, [(i, i ^ mask) for i in range(size)])


def passed_states(message, axis, size, ahead, name):
    inside = jnp.zeros_like(message)
    mask = 1
    while True:
        other = swap_with(message, axis, size, mask)
        if mask * 2 >= size:
            return mask, inside, other
        first = mask == 1
        message, inside = call(
            functools.partial(combine_kernel, first, mask, ahead),
            (shape(message.shape), shape(message.shape)),
            name=name,
        )(message, other, *([] if first else [inside]))
        mask *= 2


def local(sizes, query, key, value, decay, out_grad, out_weight):
    tm, fsdp = sizes
    rows, lanes = query.shape
    heads = lanes // HEAD_DIM
    blocks = rows // BLOCK
    direct = tm == fsdp and tm & (tm - 1) == 0

    order = {0: out_grad}
    mask = fsdp // 2
    while mask:
        for held in list(order):
            order[held | mask] = swap_with(order[held], "fsdp", fsdp, mask)
        mask //= 2
    columns = [order[j] for j in range(fsdp)]

    if direct:
        weights = [out_weight] + [swap_with(out_weight, "tm", tm, k) for k in range(1, tm)]
    else:
        whole = lax.all_gather(out_weight, "tm", axis=1, tiled=True)
        weights = jnp.split(whole, fsdp, axis=1)

    crow_shape = shape((blocks, PAD, BLOCK))
    message_shape = shape((HEAD_DIM + PAD, lanes))
    crow, ccol, state_blocks, message = call(
        functools.partial(summary_kernel, heads, blocks),
        (
            crow_shape,
            shape((BLOCK, blocks * PAD)),
            shape((blocks, HEAD_DIM, lanes)),
            message_shape,
        ),
        name="summary",
    )(decay.T, key, value)
    mask, before, other = passed_states(message, "tm", tm, True, "combine_ahead")
    inside = call(
        functools.partial(inside_kernel, heads, blocks), shape((rows, lanes)), name="inside"
    )(query, key, value, crow, ccol)
    out_t, states = call(
        functools.partial(output_kernel, heads, blocks, mask),
        (shape((lanes, rows), BF16), shape((blocks + 1, HEAD_DIM, lanes))),
        name="outputs",
    )(query, ccol, inside, before, other, state_blocks)

    width = out_grad.shape[1]
    sent = BF16 if direct else F32
    partials = call(
        lambda *refs: weight_kernel(fsdp, direct, refs),
        tuple(shape((lanes, width), F32 if k == 0 else sent) for k in range(fsdp)),
        scratch=[pltpu.VMEM((fsdp, lanes, width), F32)],
        name="weight",
    )(out_t, *columns)
    if direct:
        weight_grad = partials[0]
        for k in range(1, tm):
            weight_grad = weight_grad + swap_with(partials[k], "tm", tm, k).astype(F32)
    else:
        weight_grad = lax.psum_scatter(
            jnp.concatenate(partials, axis=1), "tm", scatter_dimension=1, tiled=True
        )

    grad_high, grad_low, back_blocks, message = call(
        lambda *refs: inner_kernel(heads, blocks, fsdp, direct, refs),
        (
            shape((rows, lanes), BF16),
            shape((rows, lanes), BF16),
            shape((blocks, HEAD_DIM, lanes)),
            message_shape,
        ),
        scratch=[pltpu.VMEM((fsdp, lanes, width), BF16), pltpu.VMEM((rows, lanes), F32)],
        name="inner",
    )(*weights, *columns, query, ccol)
    mask, before, other = passed_states(message, "tm", tm, False, "combine_back")

    query_grad, query_terms, key_inside, value_inside = call(
        functools.partial(grads_kernel, heads, blocks),
        (shape((rows, lanes), BF16), crow_shape, shape((rows, lanes)), shape((rows, lanes))),
        name="grads",
    )(query, key, value, grad_high, grad_low, crow, ccol, states)
    key_grad, value_grad, decay_grad = call(
        functools.partial(final_kernel, heads, blocks, mask),
        (shape((rows, lanes), BF16), shape((rows, lanes), BF16), shape((heads, rows))),
        scratch=[
            pltpu.VMEM((blocks, PAD, BLOCK), F32),
            pltpu.VMEM((blocks, PAD, lanes), F32),
        ],
        name="final",
    )(
        key, value, ccol, states, before, other, back_blocks, query_terms, key_inside,
        value_inside,
    )
    return query_grad, key_grad, value_grad, decay_grad.T, weight_grad


def solution(mesh):
    wide = P(("groups", "tm"), "fsdp")
    sizes = (mesh.shape["tm"], mesh.shape["fsdp"])
    return jax.shard_map(
        functools.partial(local, sizes),
        mesh=mesh,
        in_specs=(wide, wide, wide, wide, wide, P("fsdp", "tm")),
        out_specs=(wide, wide, wide, wide, P(("groups", "fsdp"), "tm")),
        check_vma=False,
    )
```

```python
import functools

import jax
import jax.numpy as jnp
from jax import lax
from jax.experimental import pallas as pl
from jax.experimental.pallas import tpu as pltpu
from jax.sharding import PartitionSpec as P


HEAD_DIM = 64
BLOCK = 128
PAD = 8
PAIR = 2 * HEAD_DIM
LOG2_E = 1.4426950408889634

F32 = jnp.float32
BF16 = jnp.bfloat16
NN = (((1,), (0,)), ((), ()))
NT = (((1,), (1,)), ((), ()))

PIECES = 2
GRANT = 24 << 20
COST = {
    "summary": 3, "inside": 4, "outputs": 3, "weight": 2, "inner": 3, "queries": 4, "sources": 4,
    "final": 4,
}


def mm(a, b, dims=NN):
    return lax.dot_general(a, b, dims, preferred_element_type=F32)


def split2(x):
    high = x.astype(BF16)
    return high, (x - high.astype(F32)).astype(BF16)


def split3(x):
    high = x.astype(BF16)
    rest = x - high.astype(F32)
    mid = rest.astype(BF16)
    return high, mid, (rest - mid.astype(F32)).astype(BF16)


def iota(shape, axis):
    return lax.broadcasted_iota(jnp.int32, shape, axis)


def ones_where(keep):
    return jnp.where(keep, 1.0, 0.0).astype(BF16)


def cat(parts, axis):
    return jnp.concatenate(parts, axis=axis)


def rows_of(b):
    return pl.ds(b * BLOCK, BLOCK)


def loop(blocks, step, carry):
    for b in range(blocks):
        carry = step(b, carry)
    return carry


def lanes_of(p):
    return slice(p * PAIR, (p + 1) * PAIR)


def first_head(like):
    return iota(like.shape, 1) < HEAD_DIM


def stacked(pair):
    keep, zero = first_head(pair), jnp.zeros_like(pair)
    return cat([jnp.where(keep, pair, zero), jnp.where(keep, zero, pair)], 0)


def spread_heads(both):
    count = both.shape[1] // PAIR
    zero = jnp.zeros((2 * both.shape[0], PAIR), both.dtype)
    out = []
    for p in range(count):
        row = [zero] * count
        row[p] = stacked(both[:, lanes_of(p)])
        out.append(cat(row, 1))
    return cat(out, 0)


def apart(pair_t):
    top, low = pair_t[:HEAD_DIM, :], pair_t[HEAD_DIM:, :]
    zero = jnp.zeros_like(top)
    return cat([cat([top, zero], 1), cat([zero, low], 1)], 0)


def turned(full):
    count = full.shape[1] // PAIR
    zero = jnp.zeros((PAIR, PAIR), full.dtype)
    out = []
    for p in range(count):
        row = [zero] * count
        row[p] = full[lanes_of(p), lanes_of(p)].T
        out.append(cat(row, 1))
    return cat(out, 0)


def compact(full):
    out = []
    for p in range(full.shape[1] // PAIR):
        mine = full[lanes_of(p), lanes_of(p)]
        top = mine[:HEAD_DIM, :]
        out.append(jnp.where(first_head(top), top, mine[HEAD_DIM:, :]))
    return cat(out, 1)


def columns_of(by_token, b):
    return by_token[:, b * PAD : (b + 1) * PAD]


def wide_all(columns, heads):
    return cat([wide_of(columns, p) for p in range(heads // 2)], 1)


def wide_of(columns, p):
    one, two = columns[:, 2 * p : 2 * p + 1], columns[:, 2 * p + 1 : 2 * p + 2]
    keep = iota((BLOCK, PAIR), 1) < HEAD_DIM
    return jnp.where(
        keep, jnp.broadcast_to(one, (BLOCK, PAIR)), jnp.broadcast_to(two, (BLOCK, PAIR))
    )


def exponents(columns, crow_block, p):
    return [
        jnp.broadcast_to(columns[:, h : h + 1], (BLOCK, BLOCK)) - crow_block[h : h + 1, :]
        for h in (2 * p, 2 * p + 1)
    ]


def pair_weights(expos, flipped):
    row, col = iota((BLOCK, BLOCK), 0), iota((BLOCK, BLOCK), 1)
    keep = (row <= col) if flipped else (row >= col)
    return cat([jnp.where(keep, jnp.exp2(-e if flipped else e), 0.0) for e in expos], 1)


def fold(both):
    half = both.shape[0] // 2
    return both[:half, :] + both[half:, :]


def wide_state(state):
    high, low = split2(state)
    return spread_heads(high), spread_heads(low)


def takes_from(mask, ahead):
    later = (lax.axis_index("tm") & mask) != 0
    return later if ahead else jnp.logical_not(later)


def entering(takes, inside, other):
    state, total = inside[:HEAD_DIM, :], inside[HEAD_DIM : HEAD_DIM + 1, :]
    return jnp.where(takes, state + jnp.exp2(total) * other[:HEAD_DIM, :], state)


def summary_kernel(
    heads, blocks, decay_far, key_far, value_far, crow, ccol, state_blocks, message,
    decay, key, value, decay_sem, sems,
):
    lanes = heads * HEAD_DIM
    first = pltpu.make_async_copy(decay_far, decay, decay_sem)
    first.start()
    copies = []
    size = key.shape[0] // PIECES
    for i in range(PIECES):
        rows = pl.ds(i * size, size)
        pair = (
            pltpu.make_async_copy(key_far.at[rows, :], key.at[rows, :], sems.at[0, i]),
            pltpu.make_async_copy(value_far.at[rows, :], value.at[rows, :], sems.at[1, i]),
        )
        for copy in pair:
            copy.start()
        copies.append(pair)
    first.wait()
    upper = ones_where(iota((BLOCK, BLOCK), 0) <= iota((BLOCK, BLOCK), 1))
    filler = [jnp.zeros((PAD - heads, BLOCK), F32)] if heads < PAD else []
    rates = cat([cat([decay[:, rows_of(b)]] + filler, 0) for b in range(blocks)], 0) * LOG2_E
    sums = mm(cat(split3(rates), 0), upper)
    size = blocks * PAD
    cum = sums[:size, :] + sums[size : 2 * size, :] + sums[2 * size :, :]
    by_token = cum.T
    ccol[...] = by_token
    state, total = jnp.zeros((HEAD_DIM, lanes), F32), jnp.zeros((1, lanes), F32)
    for b in range(blocks):
        rows = rows_of(b)
        if b * PIECES % blocks == 0:
            for copy in copies[b * PIECES // blocks]:
                copy.wait()
        crow[b] = cum[b * PAD : (b + 1) * PAD, :]
        columns = columns_of(by_token, b)
        wide = wide_all(columns, heads)
        block_total = wide[BLOCK - 1 :, :]
        shrunk = value[rows, :].astype(F32) * jnp.exp2(block_total - wide)
        key_t = key[rows, :].T
        block_state = compact(mm(cat([key_t, key_t], 1), cat(split2(shrunk), 0)))
        state_blocks[b] = block_state
        state = jnp.exp2(block_total) * state + block_state
        total = total + block_total
    message[:HEAD_DIM, :] = state
    message[HEAD_DIM:, :] = jnp.broadcast_to(total, (PAD, lanes))


def inside_kernel(
    heads, blocks, query, key, value, crow, ccol, out, later, earlier, scores_high, scores_low
):
    def step(b, carry):
        rows = rows_of(b)
        crow_block = crow[b]
        columns = columns_of(ccol, b)
        q, k = query[rows, :], key[rows, :]
        scores, scores_t = [], []
        for p in range(heads // 2):
            side = lanes_of(p)
            across = slice(2 * p * BLOCK, 2 * (p + 1) * BLOCK)
            expos = exponents(columns, crow_block, p)
            weights, flipped = pair_weights(expos, False), pair_weights(expos, True)
            later[rows, across] = weights
            earlier[rows, across] = flipped
            scores.append(mm(q[:, side], apart(k[:, side].T)) * weights)
            scores_t.append(mm(k[:, side], apart(q[:, side].T)) * flipped)
        out[rows, :] = fold(mm(cat(split2(cat(scores, 1)), 0), spread_heads(value[rows, :])))
        high, low = split2(cat(scores_t, 1))
        scores_high[rows, :] = high
        scores_low[rows, :] = low
        return carry

    loop(blocks, step, 0)


def output_kernel(
    heads, blocks, mask, query, ccol, inside, before, other, state_blocks, out_t, states
):
    def step(b, state):
        rows = rows_of(b)
        states[b] = state
        columns = columns_of(ccol, b)
        wide = wide_all(columns, heads)
        q = query[rows, :]
        carried = mm(cat([q, q], 1), cat(wide_state(state), 0))
        block_out = (inside[rows, :] + jnp.exp2(wide) * carried).astype(BF16)
        out_t[:, rows] = block_out.T
        return jnp.exp2(wide[BLOCK - 1 :, :]) * state + state_blocks[b]

    first = entering(takes_from(mask, True), before, other)
    states[blocks] = loop(blocks, step, first)


def swap_of(direct):
    column = lax.axis_index("fsdp")
    return lax.axis_index("tm") ^ column if direct else column


def inner_kernel(heads, blocks, count, direct, swapped, refs):
    swap = swap_of(direct)
    weights = refs[:count]
    columns_in = refs[count : 2 * count]
    query, ccol, grad_high, grad_low, back_blocks, message, held, total = refs[2 * count :]
    lanes = heads * HEAD_DIM
    for k in range(count):
        if swapped and k >= 2:
            held[k ^ lax.axis_index("groups")] = weights[k][...]
        else:
            held[k] = weights[k][...]
    for j in range(count):
        part = mm(columns_in[j][...], held[swap ^ j], NT)
        total[...] = part if j == 0 else total[...] + part

    def step(i, carry):
        back, decayed = carry
        b = blocks - 1 - i
        rows = rows_of(b)
        columns = columns_of(ccol, b)
        wide = wide_all(columns, heads)
        block_total = wide[BLOCK - 1 :, :]
        grad = total[rows, :]
        high, low = split2(grad)
        grad_high[rows, :] = high
        grad_low[rows, :] = low
        query_t = query[rows, :].T
        grown = split2(grad * jnp.exp2(wide))
        block_back = compact(mm(cat([query_t, query_t], 1), cat(grown, 0)))
        back_blocks[b] = block_back
        return jnp.exp2(block_total) * back + block_back, decayed + block_total

    carry = (jnp.zeros((HEAD_DIM, lanes), F32), jnp.zeros((1, lanes), F32))
    back, decayed = loop(blocks, step, carry)
    message[:HEAD_DIM, :] = back
    message[HEAD_DIM:, :] = jnp.broadcast_to(decayed, (PAD, lanes))


def weight_kernel(count, direct, refs):
    swap = swap_of(direct)
    out_t = refs[0]
    columns = refs[1 : 1 + count]
    outs = refs[1 + count : 1 + 2 * count]
    held = refs[1 + 2 * count]
    for j in range(count):
        held[j] = mm(out_t[...], columns[j][...])
    for k in range(count):
        outs[k][...] = held[swap ^ k].astype(outs[k].dtype)


def head_columns(terms, b, blocks):
    lanes, width = terms.shape[1], blocks * PAD
    pick = ones_where(
        iota((lanes, width), 0) // HEAD_DIM + b * PAD == iota((lanes, width), 1)
    )
    return fold(mm(cat(split2(terms), 0), pick))


def query_kernel(
    heads, blocks, query, key, value, grad_high, grad_low, ccol, states, later,
    query_grad, query_terms,
):
    def step(b, carry):
        rows = rows_of(b)
        k, v = key[rows, :], value[rows, :]
        gh, gl = grad_high[rows, :], grad_low[rows, :]
        scores = []
        for p in range(heads // 2):
            side = lanes_of(p)
            v_apart = apart(v[:, side].T)
            both = cat([gh[:, side], gl[:, side]], 1)
            scores.append(mm(both, cat([v_apart, v_apart], 0)))
        weighed = split2(cat(scores, 1) * later[rows, :])
        state_high, state_low = wide_state(states[b])
        carried = fold(mm(cat([gh, gl], 0), turned(state_high))) + mm(gh, turned(state_low))
        full = jnp.exp2(wide_all(columns_of(ccol, b), heads)) * carried
        full = full + fold(mm(cat(weighed, 0), spread_heads(k)))
        query_grad[rows, :] = full.astype(BF16)
        return carry + head_columns(query[rows, :].astype(F32) * full, b, blocks)

    query_terms[...] = loop(blocks, step, jnp.zeros((BLOCK, blocks * PAD), F32))


def source_kernel(
    heads, blocks, query, value, grad_high, grad_low, earlier, scores_high, scores_low,
    key_inside, value_inside,
):
    def step(b, carry):
        rows = rows_of(b)
        v = value[rows, :]
        gh, gl = grad_high[rows, :], grad_low[rows, :]
        scores = []
        for p in range(heads // 2):
            side = lanes_of(p)
            both = cat([apart(gh[:, side].T), apart(gl[:, side].T)], 0)
            scores.append(mm(cat([v[:, side], v[:, side]], 1), both))
        weighed = split2(cat(scores, 1) * earlier[rows, :])
        high, low = scores_high[rows, :], scores_low[rows, :]
        value_inside[rows, :] = fold(mm(cat([high, low], 0), spread_heads(gh))) + mm(
            high, spread_heads(gl)
        )
        key_inside[rows, :] = fold(mm(cat(weighed, 0), spread_heads(query[rows, :])))
        return carry

    loop(blocks, step, 0)


def final_kernel(
    heads, blocks, mask, key, value, ccol, states, before, other, back_blocks, query_terms,
    key_inside, value_inside, *rest,
):
    parts, (key_grad, value_grad, decay_grad, weight_grad, tail_rows) = rest[:-5], rest[-5:]
    lanes = heads * HEAD_DIM
    weight_grad[...] = sum(part[...].astype(F32) for part in parts)

    def step(i, carry):
        back, terms = carry
        b = blocks - 1 - i
        rows = rows_of(b)
        columns = columns_of(ccol, b)
        k, v = key[rows, :], value[rows, :]
        wide = wide_all(columns, heads)
        block_total = wide[BLOCK - 1 :, :]
        shrink = jnp.exp2(block_total - wide)
        back_high, back_low = wide_state(back)
        carried = mm(cat([v, v], 1), cat([turned(back_high), turned(back_low)], 0))
        key_full = key_inside[rows, :] + shrink * carried
        carried = mm(cat([k, k], 1), cat([back_high, back_low], 0))
        value_full = value_inside[rows, :] + shrink * carried
        key_grad[rows, :] = key_full.astype(BF16)
        value_grad[rows, :] = value_full.astype(BF16)
        terms = terms - head_columns(k.astype(F32) * key_full, b, blocks)
        tail_rows[b] = jnp.broadcast_to(
            jnp.sum(states[b + 1] * back, axis=0, keepdims=True), (PAD, lanes)
        )
        return jnp.exp2(block_total) * back + back_blocks[b], terms

    first = entering(takes_from(mask, False), before, other)
    _, terms = loop(blocks, step, (first, query_terms[...]))
    lower = ones_where(iota((BLOCK, BLOCK), 0) >= iota((BLOCK, BLOCK), 1))
    sums = mm(cat(split3(terms.T), 0), lower)
    size = blocks * PAD
    sums = sums[:size, :] + sums[size : 2 * size, :] + sums[2 * size :, :]
    tails = cat([tail_rows[b] for b in range(blocks)], 0)
    pick = ones_where(iota((PAD, lanes), 1) // HEAD_DIM == iota((PAD, lanes), 0))
    ends = sum(mm(pick, part, NT) for part in split3(tails))
    for b in range(blocks):
        end = jnp.broadcast_to(ends[:, b * PAD : b * PAD + 1], (PAD, BLOCK))
        both = sums[b * PAD : (b + 1) * PAD, :] + end
        decay_grad[:, rows_of(b)] = both[:heads, :]


def combine_kernel(first, mask, ahead, mine, other, *refs):
    inside = None if first else refs[0]
    sent, kept = refs[-2:]
    takes = takes_from(mask, ahead)
    group, total = mine[:HEAD_DIM, :], mine[HEAD_DIM:, :]
    other_group, other_total = other[:HEAD_DIM, :], other[HEAD_DIM:, :]
    if first:
        state, decayed = jnp.zeros_like(group), jnp.zeros_like(total)
    else:
        state, decayed = inside[:HEAD_DIM, :], inside[HEAD_DIM:, :]
    kept[:HEAD_DIM, :] = jnp.where(takes, state + jnp.exp2(decayed[:1, :]) * other_group, state)
    kept[HEAD_DIM:, :] = jnp.where(takes, decayed + other_total, decayed)
    sent[:HEAD_DIM, :] = jnp.where(
        takes,
        jnp.exp2(total[:1, :]) * other_group + group,
        jnp.exp2(other_total[:1, :]) * group + other_group,
    )
    sent[HEAD_DIM:, :] = total + other_total


def shape(dims, dtype=F32):
    return jax.ShapeDtypeStruct(dims, dtype)


def call(kernel, outs, scratch=(), name=None, far=False):
    def run(*args):
        vmem = pl.BlockSpec(memory_space=pltpu.VMEM)
        return pl.pallas_call(
            kernel,
            out_shape=outs,
            in_specs=[pl.BlockSpec(memory_space=pltpu.HBM) if far else vmem] * len(args),
            out_specs=jax.tree.map(lambda _: vmem, outs),
            scratch_shapes=list(scratch),
            compiler_params=pltpu.CompilerParams(vmem_limit_bytes=GRANT),
            cost_estimate=pl.CostEstimate(
                flops=COST.get(name, 1) * 1_000_000_000, bytes_accessed=0, transcendentals=0
            ),
        )(*args)

    return run


def swap_with(value, axis, size, mask):
    return lax.ppermute(value, axis, [(i, i ^ mask) for i in range(size)])


def passed_states(message, axis, size, ahead, name):
    inside = jnp.zeros_like(message)
    mask = 1
    while True:
        other = swap_with(message, axis, size, mask)
        if mask * 2 >= size:
            return mask, inside, other
        first = mask == 1
        message, inside = call(
            functools.partial(combine_kernel, first, mask, ahead),
            (shape(message.shape), shape(message.shape)),
            name=name,
        )(message, other, *([] if first else [inside]))
        mask *= 2


def crossed(groups, tm):
    return groups == 2 and tm == 4


def gathered_shares(share, groups, tm):
    out = [share]
    for k in range(1, 2 if crossed(groups, tm) else tm):
        out.append(swap_with(share, "tm", tm, k))
    if crossed(groups, tm):
        pairs = [(g * tm + i, g * tm + (i ^ (2 + g))) for g in range(groups) for i in range(tm)]
        out.append(lax.ppermute(share, ("groups", "tm"), pairs))
        out.append(swap_with(out[-1], "groups", groups, 1))
    return out


def local(sizes, query, key, value, decay, out_grad, out_weight):
    groups, tm, fsdp = sizes
    rows, lanes = query.shape
    heads = lanes // HEAD_DIM
    blocks = rows // BLOCK
    direct = tm == fsdp and tm & (tm - 1) == 0

    order = {0: out_grad}
    mask = fsdp // 2
    while mask:
        for held in list(order):
            order[held | mask] = swap_with(order[held], "fsdp", fsdp, mask)
        mask //= 2
    columns = [order[j] for j in range(fsdp)]

    if direct:
        weights = gathered_shares(out_weight, groups, tm)
    else:
        whole = lax.all_gather(out_weight, "tm", axis=1, tiled=True)
        weights = jnp.split(whole, fsdp, axis=1)

    crow_shape = shape((blocks, PAD, BLOCK))
    message_shape = shape((HEAD_DIM + PAD, lanes))
    crow, ccol, state_blocks, message = call(
        functools.partial(summary_kernel, heads, blocks),
        (
            crow_shape,
            shape((BLOCK, blocks * PAD)),
            shape((blocks, HEAD_DIM, lanes)),
            message_shape,
        ),
        scratch=[
            pltpu.VMEM((heads, rows), F32),
            pltpu.VMEM((rows, lanes), BF16),
            pltpu.VMEM((rows, lanes), BF16),
            pltpu.SemaphoreType.DMA(()),
            pltpu.SemaphoreType.DMA((2, PIECES)),
        ],
        name="summary",
        far=True,
    )(*(pltpu.with_memory_space_constraint(x, pltpu.HBM) for x in (decay.T, key, value)))
    mask, before, other = passed_states(message, "tm", tm, True, "combine_ahead")
    pairs = heads * BLOCK
    inside, later, earlier, scores_high, scores_low = call(
        functools.partial(inside_kernel, heads, blocks),
        (
            shape((rows, lanes)),
            shape((rows, pairs)),
            shape((rows, pairs)),
            shape((rows, pairs), BF16),
            shape((rows, pairs), BF16),
        ),
        name="inside",
    )(query, key, value, crow, ccol)
    out_t, states = call(
        functools.partial(output_kernel, heads, blocks, mask),
        (shape((lanes, rows), BF16), shape((blocks + 1, HEAD_DIM, lanes))),
        name="outputs",
    )(query, ccol, inside, before, other, state_blocks)

    width = out_grad.shape[1]
    sent = BF16 if direct else F32
    partials = call(
        lambda *refs: weight_kernel(fsdp, direct, refs),
        tuple(shape((lanes, width), F32 if k == 0 else sent) for k in range(fsdp)),
        scratch=[pltpu.VMEM((fsdp, lanes, width), F32)],
        name="weight",
    )(out_t, *columns)
    if direct:
        received = []
        for k in range(1, tm):
            received.append(swap_with(partials[k], "tm", tm, k))
    else:
        partials = [
            lax.psum_scatter(
                jnp.concatenate(partials, axis=1), "tm", scatter_dimension=1, tiled=True
            )
        ]
        received = []

    grad_high, grad_low, back_blocks, message = call(
        lambda *refs: inner_kernel(heads, blocks, fsdp, direct, direct and crossed(groups, tm), refs),
        (
            shape((rows, lanes), BF16),
            shape((rows, lanes), BF16),
            shape((blocks, HEAD_DIM, lanes)),
            message_shape,
        ),
        scratch=[pltpu.VMEM((fsdp, lanes, width), BF16), pltpu.VMEM((rows, lanes), F32)],
        name="inner",
    )(*weights, *columns, query, ccol)
    mask, before, other = passed_states(message, "tm", tm, False, "combine_back")

    query_grad, query_terms = call(
        functools.partial(query_kernel, heads, blocks),
        (shape((rows, lanes), BF16), shape((BLOCK, blocks * PAD))),
        name="queries",
    )(query, key, value, grad_high, grad_low, ccol, states, later)
    key_inside, value_inside = call(
        functools.partial(source_kernel, heads, blocks),
        (shape((rows, lanes)), shape((rows, lanes))),
        name="sources",
    )(query, value, grad_high, grad_low, earlier, scores_high, scores_low)
    key_grad, value_grad, decay_grad, weight_grad = call(
        functools.partial(final_kernel, heads, blocks, mask),
        (
            shape((rows, lanes), BF16),
            shape((rows, lanes), BF16),
            shape((heads, rows)),
            shape(partials[0].shape),
        ),
        scratch=[pltpu.VMEM((blocks, PAD, lanes), F32)],
        name="final",
    )(
        key, value, ccol, states, before, other, back_blocks, query_terms, key_inside,
        value_inside, partials[0], *received,
    )
    return query_grad, key_grad, value_grad, decay_grad.T, weight_grad


def solution(mesh):
    wide = P(("groups", "tm"), "fsdp")
    sizes = (mesh.shape["groups"], mesh.shape["tm"], mesh.shape["fsdp"])

    def body(*args):
        return local(sizes, *args)

    return jax.shard_map(
        body,
        mesh=mesh,
        in_specs=(wide, wide, wide, wide, wide, P("fsdp", "tm")),
        out_specs=(wide, wide, wide, wide, P(("groups", "fsdp"), "tm")),
        check_vma=False,
    )
```

```python
import functools

import jax
import jax.numpy as jnp
from jax import lax
from jax.experimental import pallas as pl
from jax.experimental.pallas import tpu as pltpu
from jax.sharding import PartitionSpec as P


HEAD_DIM = 64
BLOCK = 128
PAD = 8
PAIR = 2 * HEAD_DIM
LOG2_E = 1.4426950408889634

F32 = jnp.float32
BF16 = jnp.bfloat16
NN = (((1,), (0,)), ((), ()))
NT = (((1,), (1,)), ((), ()))

PIECES = 2
GRANT = 24 << 20
COST = {
    "summary": 3, "inside": 4, "outputs": 3, "weight": 2, "inner": 3, "queries": 4, "sources": 4,
    "final": 4,
}


def mm(a, b, dims=NN):
    return lax.dot_general(a, b, dims, preferred_element_type=F32)


def split2(x):
    high = x.astype(BF16)
    return high, (x - high.astype(F32)).astype(BF16)


def split3(x):
    high = x.astype(BF16)
    rest = x - high.astype(F32)
    mid = rest.astype(BF16)
    return high, mid, (rest - mid.astype(F32)).astype(BF16)


def iota(shape, axis):
    return lax.broadcasted_iota(jnp.int32, shape, axis)


def ones_where(keep):
    return jnp.where(keep, 1.0, 0.0).astype(BF16)


def cat(parts, axis):
    return jnp.concatenate(parts, axis=axis)


def rows_of(b):
    return pl.ds(b * BLOCK, BLOCK)


def loop(blocks, step, carry):
    for b in range(blocks):
        carry = step(b, carry)
    return carry


def lanes_of(p):
    return slice(p * PAIR, (p + 1) * PAIR)


def first_head(like):
    return iota(like.shape, 1) < HEAD_DIM


def stacked(pair):
    keep, zero = first_head(pair), jnp.zeros_like(pair)
    return cat([jnp.where(keep, pair, zero), jnp.where(keep, zero, pair)], 0)


def spread_heads(both):
    count = both.shape[1] // PAIR
    zero = jnp.zeros((2 * both.shape[0], PAIR), both.dtype)
    out = []
    for p in range(count):
        row = [zero] * count
        row[p] = stacked(both[:, lanes_of(p)])
        out.append(cat(row, 1))
    return cat(out, 0)


def apart(pair_t):
    top, low = pair_t[:HEAD_DIM, :], pair_t[HEAD_DIM:, :]
    zero = jnp.zeros_like(top)
    return cat([cat([top, zero], 1), cat([zero, low], 1)], 0)


def turned(full):
    count = full.shape[1] // PAIR
    zero = jnp.zeros((PAIR, PAIR), full.dtype)
    out = []
    for p in range(count):
        row = [zero] * count
        row[p] = full[lanes_of(p), lanes_of(p)].T
        out.append(cat(row, 1))
    return cat(out, 0)


def compact(full):
    out = []
    for p in range(full.shape[1] // PAIR):
        mine = full[lanes_of(p), lanes_of(p)]
        top = mine[:HEAD_DIM, :]
        out.append(jnp.where(first_head(top), top, mine[HEAD_DIM:, :]))
    return cat(out, 1)


def columns_of(by_token, b):
    return by_token[:, b * PAD : (b + 1) * PAD]


def wide_all(columns, heads):
    return cat([wide_of(columns, p) for p in range(heads // 2)], 1)


def wide_of(columns, p):
    one, two = columns[:, 2 * p : 2 * p + 1], columns[:, 2 * p + 1 : 2 * p + 2]
    keep = iota((BLOCK, PAIR), 1) < HEAD_DIM
    return jnp.where(
        keep, jnp.broadcast_to(one, (BLOCK, PAIR)), jnp.broadcast_to(two, (BLOCK, PAIR))
    )


def exponents(columns, crow_block, p):
    return [
        jnp.broadcast_to(columns[:, h : h + 1], (BLOCK, BLOCK)) - crow_block[h : h + 1, :]
        for h in (2 * p, 2 * p + 1)
    ]


def pair_weights(expos, flipped):
    row, col = iota((BLOCK, BLOCK), 0), iota((BLOCK, BLOCK), 1)
    keep = (row <= col) if flipped else (row >= col)
    return cat([jnp.where(keep, jnp.exp2(-e if flipped else e), 0.0) for e in expos], 1)


def fold(both):
    half = both.shape[0] // 2
    return both[:half, :] + both[half:, :]


def wide_state(state):
    high, low = split2(state)
    return spread_heads(high), spread_heads(low)


def takes_from(mask, ahead):
    later = (lax.axis_index("tm") & mask) != 0
    return later if ahead else jnp.logical_not(later)


def entering(takes, inside, other):
    state, total = inside[:HEAD_DIM, :], inside[HEAD_DIM : HEAD_DIM + 1, :]
    return jnp.where(takes, state + jnp.exp2(total) * other[:HEAD_DIM, :], state)


def summary_kernel(
    heads, blocks, decay_far, key_far, value_far, crow, ccol, state_blocks, message,
    decay, key, value, decay_sem, sems,
):
    lanes = heads * HEAD_DIM
    first = pltpu.make_async_copy(decay_far, decay, decay_sem)
    first.start()
    copies = []
    size = key.shape[0] // PIECES
    for i in range(PIECES):
        rows = pl.ds(i * size, size)
        pair = (
            pltpu.make_async_copy(key_far.at[rows, :], key.at[rows, :], sems.at[0, i]),
            pltpu.make_async_copy(value_far.at[rows, :], value.at[rows, :], sems.at[1, i]),
        )
        for copy in pair:
            copy.start()
        copies.append(pair)
    first.wait()
    upper = ones_where(iota((BLOCK, BLOCK), 0) <= iota((BLOCK, BLOCK), 1))
    filler = [jnp.zeros((PAD - heads, BLOCK), F32)] if heads < PAD else []
    rates = cat([cat([decay[:, rows_of(b)]] + filler, 0) for b in range(blocks)], 0) * LOG2_E
    sums = mm(cat(split3(rates), 0), upper)
    size = blocks * PAD
    cum = sums[:size, :] + sums[size : 2 * size, :] + sums[2 * size :, :]
    by_token = cum.T
    ccol[...] = by_token
    state, total = jnp.zeros((HEAD_DIM, lanes), F32), jnp.zeros((1, lanes), F32)
    for b in range(blocks):
        rows = rows_of(b)
        if b * PIECES % blocks == 0:
            for copy in copies[b * PIECES // blocks]:
                copy.wait()
        crow[b] = cum[b * PAD : (b + 1) * PAD, :]
        columns = columns_of(by_token, b)
        wide = wide_all(columns, heads)
        block_total = wide[BLOCK - 1 :, :]
        shrunk = value[rows, :].astype(F32) * jnp.exp2(block_total - wide)
        key_t = key[rows, :].T
        block_state = compact(mm(cat([key_t, key_t], 1), cat(split2(shrunk), 0)))
        state_blocks[b] = block_state
        state = jnp.exp2(block_total) * state + block_state
        total = total + block_total
    message[:HEAD_DIM, :] = state
    message[HEAD_DIM:, :] = jnp.broadcast_to(total, (PAD, lanes))


def inside_kernel(
    heads, blocks, query, key, value, crow, ccol, out, later, earlier, scores_high, scores_low
):
    def step(b, carry):
        rows = rows_of(b)
        crow_block = crow[b]
        columns = columns_of(ccol, b)
        q, k = query[rows, :], key[rows, :]
        scores, scores_t = [], []
        for p in range(heads // 2):
            side = lanes_of(p)
            across = slice(2 * p * BLOCK, 2 * (p + 1) * BLOCK)
            expos = exponents(columns, crow_block, p)
            weights, flipped = pair_weights(expos, False), pair_weights(expos, True)
            later[rows, across] = weights
            earlier[rows, across] = flipped
            scores.append(mm(q[:, side], apart(k[:, side].T)) * weights)
            scores_t.append(mm(k[:, side], apart(q[:, side].T)) * flipped)
        out[rows, :] = fold(mm(cat(split2(cat(scores, 1)), 0), spread_heads(value[rows, :])))
        high, low = split2(cat(scores_t, 1))
        scores_high[rows, :] = high
        scores_low[rows, :] = low
        return carry

    loop(blocks, step, 0)


def output_kernel(
    heads, blocks, mask, query, ccol, inside, before, other, state_blocks, out_t, states
):
    def step(b, state):
        rows = rows_of(b)
        states[b] = state
        columns = columns_of(ccol, b)
        wide = wide_all(columns, heads)
        q = query[rows, :]
        carried = mm(cat([q, q], 1), cat(wide_state(state), 0))
        block_out = (inside[rows, :] + jnp.exp2(wide) * carried).astype(BF16)
        out_t[:, rows] = block_out.T
        return jnp.exp2(wide[BLOCK - 1 :, :]) * state + state_blocks[b]

    first = entering(takes_from(mask, True), before, other)
    states[blocks] = loop(blocks, step, first)


def swap_of(direct):
    column = lax.axis_index("fsdp")
    return lax.axis_index("tm") ^ column if direct else column


def inner_kernel(heads, blocks, count, direct, swapped, refs):
    swap = swap_of(direct)
    weights = refs[:count]
    columns_in = refs[count : 2 * count]
    query, ccol, grad_high, grad_low, back_blocks, message, held, total = refs[2 * count :]
    lanes = heads * HEAD_DIM
    for k in range(count):
        if swapped and k >= 2:
            held[k ^ lax.axis_index("groups")] = weights[k][...]
        else:
            held[k] = weights[k][...]
    for j in range(count):
        part = mm(columns_in[j][...], held[swap ^ j], NT)
        total[...] = part if j == 0 else total[...] + part

    def step(i, carry):
        back, decayed = carry
        b = blocks - 1 - i
        rows = rows_of(b)
        columns = columns_of(ccol, b)
        wide = wide_all(columns, heads)
        block_total = wide[BLOCK - 1 :, :]
        grad = total[rows, :]
        high, low = split2(grad)
        grad_high[rows, :] = high
        grad_low[rows, :] = low
        query_t = query[rows, :].T
        grown = split2(grad * jnp.exp2(wide))
        block_back = compact(mm(cat([query_t, query_t], 1), cat(grown, 0)))
        back_blocks[b] = block_back
        return jnp.exp2(block_total) * back + block_back, decayed + block_total

    carry = (jnp.zeros((HEAD_DIM, lanes), F32), jnp.zeros((1, lanes), F32))
    back, decayed = loop(blocks, step, carry)
    message[:HEAD_DIM, :] = back
    message[HEAD_DIM:, :] = jnp.broadcast_to(decayed, (PAD, lanes))


def weight_kernel(count, direct, refs):
    swap = swap_of(direct)
    out_t = refs[0]
    columns = refs[1 : 1 + count]
    outs = refs[1 + count : 1 + 2 * count]
    held = refs[1 + 2 * count]
    for j in range(count):
        held[j] = mm(out_t[...], columns[j][...])
    for k in range(count):
        outs[k][...] = held[swap ^ k].astype(outs[k].dtype)


def head_columns(terms, b, blocks):
    lanes, width = terms.shape[1], blocks * PAD
    pick = ones_where(
        iota((lanes, width), 0) // HEAD_DIM + b * PAD == iota((lanes, width), 1)
    )
    return fold(mm(cat(split2(terms), 0), pick))


def query_kernel(
    heads, blocks, query, key, value, grad_high, grad_low, ccol, states, later,
    query_grad, query_terms,
):
    def step(b, carry):
        rows = rows_of(b)
        k, v = key[rows, :], value[rows, :]
        gh, gl = grad_high[rows, :], grad_low[rows, :]
        scores = []
        for p in range(heads // 2):
            side = lanes_of(p)
            v_apart = apart(v[:, side].T)
            both = cat([gh[:, side], gl[:, side]], 1)
            scores.append(mm(both, cat([v_apart, v_apart], 0)))
        weighed = split2(cat(scores, 1) * later[rows, :])
        state_high, state_low = wide_state(states[b])
        carried = fold(mm(cat([gh, gl], 0), turned(state_high))) + mm(gh, turned(state_low))
        full = jnp.exp2(wide_all(columns_of(ccol, b), heads)) * carried
        full = full + fold(mm(cat(weighed, 0), spread_heads(k)))
        query_grad[rows, :] = full.astype(BF16)
        return carry + head_columns(query[rows, :].astype(F32) * full, b, blocks)

    query_terms[...] = loop(blocks, step, jnp.zeros((BLOCK, blocks * PAD), F32))


def source_kernel(
    heads, blocks, query, value, grad_high, grad_low, ccol, earlier, scores_high, scores_low,
    key_inside, value_inside, shrinks, leaving,
):
    def step(b, carry):
        rows = rows_of(b)
        wide = wide_all(columns_of(ccol, b), heads)
        block_total = wide[BLOCK - 1 :, :]
        shrinks[rows, :] = jnp.exp2(block_total - wide)
        leaving[b] = jnp.broadcast_to(jnp.exp2(block_total), (PAD, wide.shape[1]))
        v = value[rows, :]
        gh, gl = grad_high[rows, :], grad_low[rows, :]
        scores = []
        for p in range(heads // 2):
            side = lanes_of(p)
            both = cat([apart(gh[:, side].T), apart(gl[:, side].T)], 0)
            scores.append(mm(cat([v[:, side], v[:, side]], 1), both))
        weighed = split2(cat(scores, 1) * earlier[rows, :])
        high, low = scores_high[rows, :], scores_low[rows, :]
        value_inside[rows, :] = fold(mm(cat([high, low], 0), spread_heads(gh))) + mm(
            high, spread_heads(gl)
        )
        key_inside[rows, :] = fold(mm(cat(weighed, 0), spread_heads(query[rows, :])))
        return carry

    loop(blocks, step, 0)


def final_kernel(
    heads, blocks, mask, key, value, shrinks, leaving, states, before, other, back_blocks, query_terms,
    key_inside, value_inside, *rest,
):
    parts, (key_grad, value_grad, decay_grad, weight_grad, tail_rows) = rest[:-5], rest[-5:]
    lanes = heads * HEAD_DIM
    weight_grad[...] = sum(part[...].astype(F32) for part in parts)

    def step(i, carry):
        back, terms = carry
        b = blocks - 1 - i
        rows = rows_of(b)
        k, v = key[rows, :], value[rows, :]
        shrink = shrinks[rows, :]
        back_high, back_low = wide_state(back)
        carried = mm(cat([v, v], 1), cat([turned(back_high), turned(back_low)], 0))
        key_full = key_inside[rows, :] + shrink * carried
        carried = mm(cat([k, k], 1), cat([back_high, back_low], 0))
        value_full = value_inside[rows, :] + shrink * carried
        key_grad[rows, :] = key_full.astype(BF16)
        value_grad[rows, :] = value_full.astype(BF16)
        terms = terms - head_columns(k.astype(F32) * key_full, b, blocks)
        tail_rows[b] = jnp.broadcast_to(
            jnp.sum(states[b + 1] * back, axis=0, keepdims=True), (PAD, lanes)
        )
        return leaving[b][:1, :] * back + back_blocks[b], terms

    first = entering(takes_from(mask, False), before, other)
    _, terms = loop(blocks, step, (first, query_terms[...]))
    lower = ones_where(iota((BLOCK, BLOCK), 0) >= iota((BLOCK, BLOCK), 1))
    sums = mm(cat(split3(terms.T), 0), lower)
    size = blocks * PAD
    sums = sums[:size, :] + sums[size : 2 * size, :] + sums[2 * size :, :]
    tails = cat([tail_rows[b] for b in range(blocks)], 0)
    pick = ones_where(iota((PAD, lanes), 1) // HEAD_DIM == iota((PAD, lanes), 0))
    ends = sum(mm(pick, part, NT) for part in split3(tails))
    for b in range(blocks):
        end = jnp.broadcast_to(ends[:, b * PAD : b * PAD + 1], (PAD, BLOCK))
        both = sums[b * PAD : (b + 1) * PAD, :] + end
        decay_grad[:, rows_of(b)] = both[:heads, :]


def combine_kernel(first, mask, ahead, mine, other, *refs):
    inside = None if first else refs[0]
    sent, kept = refs[-2:]
    takes = takes_from(mask, ahead)
    group, total = mine[:HEAD_DIM, :], mine[HEAD_DIM:, :]
    other_group, other_total = other[:HEAD_DIM, :], other[HEAD_DIM:, :]
    if first:
        state, decayed = jnp.zeros_like(group), jnp.zeros_like(total)
    else:
        state, decayed = inside[:HEAD_DIM, :], inside[HEAD_DIM:, :]
    kept[:HEAD_DIM, :] = jnp.where(takes, state + jnp.exp2(decayed[:1, :]) * other_group, state)
    kept[HEAD_DIM:, :] = jnp.where(takes, decayed + other_total, decayed)
    sent[:HEAD_DIM, :] = jnp.where(
        takes,
        jnp.exp2(total[:1, :]) * other_group + group,
        jnp.exp2(other_total[:1, :]) * group + other_group,
    )
    sent[HEAD_DIM:, :] = total + other_total


def shape(dims, dtype=F32):
    return jax.ShapeDtypeStruct(dims, dtype)


def call(kernel, outs, scratch=(), name=None, far=False):
    def run(*args):
        vmem = pl.BlockSpec(memory_space=pltpu.VMEM)
        return pl.pallas_call(
            kernel,
            out_shape=outs,
            in_specs=[pl.BlockSpec(memory_space=pltpu.HBM) if far else vmem] * len(args),
            out_specs=jax.tree.map(lambda _: vmem, outs),
            scratch_shapes=list(scratch),
            compiler_params=pltpu.CompilerParams(vmem_limit_bytes=GRANT),
            cost_estimate=pl.CostEstimate(
                flops=COST.get(name, 1) * 1_000_000_000, bytes_accessed=0, transcendentals=0
            ),
        )(*args)

    return run


def swap_with(value, axis, size, mask):
    return lax.ppermute(value, axis, [(i, i ^ mask) for i in range(size)])


def passed_states(message, axis, size, ahead, name):
    inside = jnp.zeros_like(message)
    mask = 1
    while True:
        other = swap_with(message, axis, size, mask)
        if mask * 2 >= size:
            return mask, inside, other
        first = mask == 1
        message, inside = call(
            functools.partial(combine_kernel, first, mask, ahead),
            (shape(message.shape), shape(message.shape)),
            name=name,
        )(message, other, *([] if first else [inside]))
        mask *= 2


def crossed(groups, tm):
    return groups == 2 and tm == 4


def gathered_shares(share, groups, tm):
    out = [share]
    for k in range(1, 2 if crossed(groups, tm) else tm):
        out.append(swap_with(share, "tm", tm, k))
    if crossed(groups, tm):
        pairs = [(g * tm + i, g * tm + (i ^ (2 + g))) for g in range(groups) for i in range(tm)]
        out.append(lax.ppermute(share, ("groups", "tm"), pairs))
        out.append(swap_with(out[-1], "groups", groups, 1))
    return out


def local(sizes, query, key, value, decay, out_grad, out_weight):
    groups, tm, fsdp = sizes
    rows, lanes = query.shape
    heads = lanes // HEAD_DIM
    blocks = rows // BLOCK
    direct = tm == fsdp and tm & (tm - 1) == 0

    order = {0: out_grad}
    mask = fsdp // 2
    while mask:
        for held in list(order):
            order[held | mask] = swap_with(order[held], "fsdp", fsdp, mask)
        mask //= 2
    columns = [order[j] for j in range(fsdp)]

    if direct:
        weights = gathered_shares(out_weight, groups, tm)
    else:
        whole = lax.all_gather(out_weight, "tm", axis=1, tiled=True)
        weights = jnp.split(whole, fsdp, axis=1)

    crow_shape = shape((blocks, PAD, BLOCK))
    message_shape = shape((HEAD_DIM + PAD, lanes))
    crow, ccol, state_blocks, message = call(
        functools.partial(summary_kernel, heads, blocks),
        (
            crow_shape,
            shape((BLOCK, blocks * PAD)),
            shape((blocks, HEAD_DIM, lanes)),
            message_shape,
        ),
        scratch=[
            pltpu.VMEM((heads, rows), F32),
            pltpu.VMEM((rows, lanes), BF16),
            pltpu.VMEM((rows, lanes), BF16),
            pltpu.SemaphoreType.DMA(()),
            pltpu.SemaphoreType.DMA((2, PIECES)),
        ],
        name="summary",
        far=True,
    )(*(pltpu.with_memory_space_constraint(x, pltpu.HBM) for x in (decay.T, key, value)))
    mask, before, other = passed_states(message, "tm", tm, True, "combine_ahead")
    pairs = heads * BLOCK
    inside, later, earlier, scores_high, scores_low = call(
        functools.partial(inside_kernel, heads, blocks),
        (
            shape((rows, lanes)),
            shape((rows, pairs)),
            shape((rows, pairs)),
            shape((rows, pairs), BF16),
            shape((rows, pairs), BF16),
        ),
        name="inside",
    )(query, key, value, crow, ccol)
    out_t, states = call(
        functools.partial(output_kernel, heads, blocks, mask),
        (shape((lanes, rows), BF16), shape((blocks + 1, HEAD_DIM, lanes))),
        name="outputs",
    )(query, ccol, inside, before, other, state_blocks)

    width = out_grad.shape[1]
    sent = BF16 if direct else F32
    partials = call(
        lambda *refs: weight_kernel(fsdp, direct, refs),
        tuple(shape((lanes, width), F32 if k == 0 else sent) for k in range(fsdp)),
        scratch=[pltpu.VMEM((fsdp, lanes, width), F32)],
        name="weight",
    )(out_t, *columns)
    if direct:
        received = []
        for k in range(1, tm):
            received.append(swap_with(partials[k], "tm", tm, k))
    else:
        partials = [
            lax.psum_scatter(
                jnp.concatenate(partials, axis=1), "tm", scatter_dimension=1, tiled=True
            )
        ]
        received = []

    grad_high, grad_low, back_blocks, message = call(
        lambda *refs: inner_kernel(heads, blocks, fsdp, direct, direct and crossed(groups, tm), refs),
        (
            shape((rows, lanes), BF16),
            shape((rows, lanes), BF16),
            shape((blocks, HEAD_DIM, lanes)),
            message_shape,
        ),
        scratch=[pltpu.VMEM((fsdp, lanes, width), BF16), pltpu.VMEM((rows, lanes), F32)],
        name="inner",
    )(*weights, *columns, query, ccol)
    mask, before, other = passed_states(message, "tm", tm, False, "combine_back")

    query_grad, query_terms = call(
        functools.partial(query_kernel, heads, blocks),
        (shape((rows, lanes), BF16), shape((BLOCK, blocks * PAD))),
        name="queries",
    )(query, key, value, grad_high, grad_low, ccol, states, later)
    key_inside, value_inside, shrinks, leaving = call(
        functools.partial(source_kernel, heads, blocks),
        (
            shape((rows, lanes)),
            shape((rows, lanes)),
            shape((rows, lanes)),
            shape((blocks, PAD, lanes)),
        ),
        name="sources",
    )(query, value, grad_high, grad_low, ccol, earlier, scores_high, scores_low)
    key_grad, value_grad, decay_grad, weight_grad = call(
        functools.partial(final_kernel, heads, blocks, mask),
        (
            shape((rows, lanes), BF16),
            shape((rows, lanes), BF16),
            shape((heads, rows)),
            shape(partials[0].shape),
        ),
        scratch=[pltpu.VMEM((blocks, PAD, lanes), F32)],
        name="final",
    )(
        key, value, shrinks, leaving, states, before, other, back_blocks, query_terms, key_inside,
        value_inside, partials[0], *received,
    )
    return query_grad, key_grad, value_grad, decay_grad.T, weight_grad


def solution(mesh):
    wide = P(("groups", "tm"), "fsdp")
    sizes = (mesh.shape["groups"], mesh.shape["tm"], mesh.shape["fsdp"])

    def body(*args):
        return local(sizes, *args)

    return jax.shard_map(
        body,
        mesh=mesh,
        in_specs=(wide, wide, wide, wide, wide, P("fsdp", "tm")),
        out_specs=(wide, wide, wide, wide, P(("groups", "fsdp"), "tm")),
        check_vma=False,
    )
```
